768 devices in a mesh: section: 2 (over core), node: 8 (over y_lo, x), dev: 48 (over z, y_hi).
Axes of the slice: x: 4, y: 8 (y_hi: 4, y_lo: 2; y = y_hi * 2 + y_lo), z: 12, core: 2. Of those that a mesh axis runs over, the one named last changes fastest.
Arguments:
- inputs_forward: bfloat16 [2, 6144, 3584], P('section', 'dev', 'node'), may hold values from -6 to 6
- routes_forward: int32 [2, 6144, 2], P('section', 'dev'), may hold values from 0 to 47, all different within a row; in each aligned block of 128 rows (0 to 127, 128 to 255, ..., all dimensions but the last counted through in order) at most 10 rows name the same one
- gates_forward: float32 [2, 6144, 2], P('section', 'dev'), may hold values from 0.2 to 1.2
- grads_backward: bfloat16 [2, 6144, 3584], P('section', 'dev', 'node'), may hold values from -6 to 6
- routes_backward: int32 [2, 6144, 2], P('section', 'dev'), may hold values from 0 to 47, all different within a row; in each aligned block of 128 rows (0 to 127, 128 to 255, ..., all dimensions but the last counted through in order) at most 10 rows name the same one
- gates_backward: float32 [2, 6144, 2], P('section', 'dev'), may hold values from 0.2 to 1.2
- w_gate: bfloat16 [2, 48, 3584, 1024], P('section', 'dev', 'node'), may hold values from -0.09375 to 0.09375
- w_up: bfloat16 [2, 48, 3584, 1024], P('section', 'dev', 'node'), may hold values from -0.09375 to 0.09375
- w_down: bfloat16 [2, 48, 1024, 3584], P('section', 'dev', None, 'node'), may hold values from -0.1875 to 0.1875
- saved_gate: bfloat16 [2, 48, 480, 1024], P('section', 'dev'), may hold values from -5 to 5
- saved_up: bfloat16 [2, 48, 480, 1024], P('section', 'dev'), may hold values from -5 to 5
Outputs:
- forward_next: bfloat16 [2, 6144, 3584], P('section', 'dev', 'node')
- backward_next: bfloat16 [2, 6144, 3584], P('section', 'dev', 'node')
The draws below stay inside these ranges and needn't reach their ends.
Inputs may be any that keep to these rules, and one draw needn't show every extreme that they name: `routes_forward`: each row names 2 different experts. Among the rows of one device no expert is named more than 10 times, a bound that some block reaches. `routes_backward`: each row names 2 different experts. Among the rows of one device no expert is named more than 10 times, a bound that some block reaches.
All inputs are finite; a program needn't handle non-finite values.
Results may differ from the reference program's by a relative error of at most 0.014.
Values may be sent and summed in bfloat16 or wider, within the bound.
A program may use at most 32 MiB of HBM per device.

```python
import math
import jax
import jax.numpy as jnp
import numpy as np
from jax import lax

D = 3584
FF = 1024
TOPK = 2
TOK_DEV = 128
EXPERTS = 48
CAP = 10
SLOTS = 480
TOKENS = 6144
N_SECTION = 2
N_NODE = 8
N_DEV = 48


def levels(rng, dims, pieces, low, largest):
    def one(dim, blocks):
        steps = jax.random.uniform(jax.random.fold_in(jax.random.fold_in(rng, 6), dim), (blocks,), jnp.float32, low / len(pieces), largest / len(pieces))
        return jnp.repeat(jnp.exp(steps), dims[dim] // blocks).reshape((-1,) + (1,) * (len(dims) - dim - 1))

    level = one(*pieces[0])
    for cut in pieces[1:]:
        level = level * one(*cut)
    return level


def shared_out(key, own, number, rows, count, top, bound, lean):
    sequence = jax.random.permutation(key, count)
    crowded, common = load_shares(count, rows * top, bound, lean, True), load_shares(count, rows * top, bound, lean, False)
    places = jnp.arange(count)

    def named(sizes, turn):
        used = int((sizes > 0).sum())
        fixed = max(1, used // 4)
        shifted = fixed + (places - fixed + turn * (used - fixed)) % max(1, count - fixed)
        return jnp.zeros((count,), jnp.int32).at[sequence[jnp.where(places < fixed, places, shifted)]].set(jnp.asarray(sizes, jnp.int32))

    sizes = jnp.where(number % 4 == 0, named(crowded, number // 4), named(common, number - number // 4 - 1))
    mixed = jax.random.permutation(jax.random.fold_in(own, 3), count)
    source_of, receiver = mixed[0:count // 2 * 2:2], mixed[1:count // 2 * 2:2]
    room = jnp.minimum(sizes[source_of] - 1, bound - sizes[receiver]) // 2
    room = jnp.where((source_of == sequence[0]) | (receiver == sequence[0]) | (sizes[receiver] == 0), 0, jnp.maximum(room, 0))
    shifted = jax.random.randint(jax.random.fold_in(own, 4), (count // 2,), 0, 1 << 20) % (room + 1)
    sizes = sizes.at[source_of].add(-shifted).at[receiver].add(shifted)
    members = jnp.searchsorted(jnp.cumsum(sizes), jnp.arange(rows * top), side="right").astype(jnp.int32)
    grid = members.reshape(top, rows).T
    grid = grid[jax.random.permutation(jax.random.fold_in(own, 1), rows)]
    turn = jax.random.randint(jax.random.fold_in(own, 2), (rows, 1), 0, top)
    return jnp.take_along_axis(grid, (jnp.arange(top)[None, :] + turn) % top, axis=1)


def load_shares(count, total, bound, slope, full):
    loads = [(1 << 20) // math.isqrt(standing ** slope) + 1 for standing in range(1, count + 1)]
    largest = bound if full else min(bound, max(-(-total // count), total * loads[0] // sum(loads)))
    least = 1 if total - largest >= count - 1 else 0
    holding, surplus = [largest] + [least] * (count - 1), total - largest - least * (count - 1)
    while surplus > 0:
        candidates = [i for i in range(1, count) if holding[i] < largest] or [i for i in range(1, count) if holding[i] < bound]
        mass, budget = sum([loads[i] for i in candidates]), surplus
        for i in candidates:
            more = min(bound - holding[i], max(1, budget * loads[i] // mass), surplus)
            holding[i] = holding[i] + more
            surplus = surplus - more
    return np.array(holding)


def centred(own_key, extent, deviation, limit, pieces=(), kind=jnp.bfloat16):
    values = deviation * jax.random.normal(own_key, extent, jnp.float32)
    if pieces:
        values = values * levels(own_key, extent, pieces, -0.22, 0.18)
    return jnp.clip(values, -limit, limit).astype(kind)


def setup_inputs(seed: int = 0) -> dict:
    streams_of = jax.random.split(jax.random.key(seed), 12)
    inputs_forward = centred(streams_of[0], (N_SECTION, TOKENS, D), 1.0, 6.0, ((0, 2), (1, 48), (2, 8)))
    routes_forward_keys = jax.random.split(jax.random.fold_in(streams_of[1], 1), N_SECTION * TOKENS // TOK_DEV)
    routes_forward_turns = jax.random.permutation(jax.random.fold_in(streams_of[1], 3), N_SECTION * TOKENS // TOK_DEV)
    routes_forward = jax.vmap(lambda own, number: shared_out(jax.random.fold_in(streams_of[1], 2), own, number, TOK_DEV, EXPERTS, TOPK, CAP, 2))(routes_forward_keys, routes_forward_turns).reshape((N_SECTION, TOKENS, TOPK))
    gates_forward = jnp.clip(jnp.exp(math.log(1.2) - 1.7917595 * jax.random.uniform(streams_of[2], (N_SECTION, TOKENS, TOPK), jnp.float32) ** levels(streams_of[2], (N_SECTION, TOKENS, TOPK), ((0, 2), (1, 48)), -0.2, 0.2)), 0.2, 1.2)
    grads_backward = centred(streams_of[3], (N_SECTION, TOKENS, D), 1.0, 6.0, ((0, 2), (1, 48), (2, 8)))
    routes_backward_keys = jax.random.split(jax.random.fold_in(streams_of[4], 1), N_SECTION * TOKENS // TOK_DEV)
    routes_backward_turns = jax.random.permutation(jax.random.fold_in(streams_of[4], 3), N_SECTION * TOKENS // TOK_DEV)
    routes_backward = jax.vmap(lambda own, number: shared_out(jax.random.fold_in(streams_of[4], 2), own, number, TOK_DEV, EXPERTS, TOPK, CAP, 2))(routes_backward_keys, routes_backward_turns).reshape((N_SECTION, TOKENS, TOPK))
    gates_backward = jnp.clip(jnp.exp(math.log(1.2) - 1.7917595 * jax.random.uniform(streams_of[5], (N_SECTION, TOKENS, TOPK), jnp.float32) ** levels(streams_of[5], (N_SECTION, TOKENS, TOPK), ((0, 2), (1, 48)), -0.2, 0.2)), 0.2, 1.2)
    w_gate = centred(streams_of[6], (N_SECTION, EXPERTS, D, FF), D ** -0.5, 0.09375, ((0, 2), (1, 48), (2, 8)))
    w_up = centred(streams_of[7], (N_SECTION, EXPERTS, D, FF), D ** -0.5, 0.09375, ((0, 2), (1, 48), (2, 8)))
    w_down = centred(streams_of[8], (N_SECTION, EXPERTS, FF, D), FF ** -0.5, 0.1875, ((0, 2), (1, 48), (3, 8)))
    saved_gate = centred(streams_of[9], (N_SECTION, EXPERTS, SLOTS, FF), 1.0, 5.0, ((0, 2), (1, 48)))
    saved_up = centred(streams_of[10], (N_SECTION, EXPERTS, SLOTS, FF), 1.0, 5.0, ((0, 2), (1, 48)))
    return {"inputs_forward": inputs_forward, "routes_forward": routes_forward, "gates_forward": gates_forward, "grads_backward": grads_backward, "routes_backward": routes_backward, "gates_backward": gates_backward, "w_gate": w_gate, "w_up": w_up, "w_down": w_down, "saved_gate": saved_gate, "saved_up": saved_up}


def slot_of(routing):
    blocks = routing.reshape(N_DEV, TOK_DEV * TOPK)
    onehot = (blocks[:, :, None] == jnp.arange(EXPERTS, dtype=jnp.int32)[None, None, :]).astype(jnp.int32)
    earlier = jnp.cumsum(onehot, axis=1) - onehot
    position = jnp.sum(earlier * onehot, axis=2)
    slots = jnp.arange(N_DEV, dtype=jnp.int32)[:, None] * CAP + position
    return blocks.reshape(-1).astype(jnp.int32), slots.reshape(-1).astype(jnp.int32)


def dispatch_rows(token_rows, experts_of, slots):
    owners = (jnp.arange(TOKENS * TOPK, dtype=jnp.int32) // TOPK).astype(jnp.int32)
    filled = jnp.zeros((EXPERTS, SLOTS, D), token_rows.dtype)
    return filled.at[experts_of, slots].set(token_rows[owners])


def block_sum(partial_value):
    rounded = lax.optimization_barrier(partial_value.astype(jnp.bfloat16))
    return jnp.sum(rounded.astype(jnp.float32), axis=0)


def expert_forward(packed):
    slot_rows, gate_matrix, up_matrix, down_matrix = packed
    blocked = slot_rows.reshape(SLOTS, N_NODE, D // N_NODE).astype(jnp.float32)
    gate_blocks = gate_matrix.reshape(N_NODE, D // N_NODE, FF).astype(jnp.float32)
    up_blocks = up_matrix.reshape(N_NODE, D // N_NODE, FF).astype(jnp.float32)
    pre_gate = block_sum(jnp.einsum("snd,ndf->nsf", blocked, gate_blocks))
    pre_up = block_sum(jnp.einsum("snd,ndf->nsf", blocked, up_blocks))
    hidden = (jax.nn.silu(pre_gate) * pre_up).astype(jnp.bfloat16)
    return jnp.dot(hidden, down_matrix, preferred_element_type=jnp.float32).astype(jnp.bfloat16)


def expert_backward(packed):
    slot_rows, gate_matrix, up_matrix, down_matrix, stored_gate, stored_up = packed
    blocked = slot_rows.reshape(SLOTS, N_NODE, D // N_NODE).astype(jnp.float32)
    down_blocks = down_matrix.reshape(FF, N_NODE, D // N_NODE).astype(jnp.float32)
    grad_hidden = block_sum(jnp.einsum("snd,fnd->nsf", blocked, down_blocks))
    act_gate = stored_gate.astype(jnp.float32)
    act_up = stored_up.astype(jnp.float32)
    squash = jax.nn.sigmoid(act_gate)
    grad_gate = (grad_hidden * act_up * squash * (1.0 + act_gate * (1.0 - squash))).astype(jnp.bfloat16)
    grad_up = (grad_hidden * act_gate * squash).astype(jnp.bfloat16)
    total = jnp.dot(grad_gate, gate_matrix.T, preferred_element_type=jnp.float32)
    total = total + jnp.dot(grad_up, up_matrix.T, preferred_element_type=jnp.float32)
    return total.astype(jnp.bfloat16)


def combine(token_rows, weights_of, slot_out, experts_of, slots):
    picked = slot_out[experts_of, slots].reshape(TOKENS, TOPK, D).astype(jnp.float32)
    mixed = token_rows.astype(jnp.float32) + jnp.sum(weights_of[:, :, None] * picked, axis=1)
    return mixed.astype(jnp.bfloat16)


def segment_work(packed):
    (token_rows, routing_forward, weights_forward, grad_rows, routing_backward, weights_backward,
     gate_matrix, up_matrix, down_matrix, stored_gate, stored_up) = packed
    experts_forward, slots_forward = slot_of(routing_forward)
    sent_forward = dispatch_rows(token_rows, experts_forward, slots_forward)
    result_forward = lax.map(expert_forward, (sent_forward, gate_matrix, up_matrix, down_matrix))
    experts_backward, slots_backward = slot_of(routing_backward)
    sent_backward = dispatch_rows(grad_rows, experts_backward, slots_backward)
    result_backward = lax.map(expert_backward, (sent_backward, gate_matrix, up_matrix, down_matrix, stored_gate, stored_up))
    forward_out = combine(token_rows, weights_forward, result_forward, experts_forward, slots_forward)
    backward_out = combine(grad_rows, weights_backward, result_backward, experts_backward, slots_backward)
    return forward_out, backward_out


def next_section(values):
    return jnp.concatenate([values[-1:], values[:-1]], axis=0)


def previous_section(values):
    return jnp.concatenate([values[1:], values[:1]], axis=0)


def reference(inputs_forward, routes_forward, gates_forward, grads_backward, routes_backward, gates_backward, w_gate, w_up, w_down, saved_gate, saved_up):
    forward_out, backward_out = lax.map(segment_work, (inputs_forward, routes_forward, gates_forward, grads_backward, routes_backward, gates_backward, w_gate, w_up, w_down, saved_gate, saved_up))
    return next_section(forward_out), previous_section(backward_out)
```

```python
import functools

import jax
import jax.numpy as jnp
from jax import lax
from jax.experimental import pallas as pl
from jax.experimental.pallas import tpu as pltpu
from jax.sharding import PartitionSpec as P

MESH = pl.DeviceIdType.MESH
BF, F32 = jnp.bfloat16, jnp.float32
HEAD, TAIL = 8, 2
CAPACITY = HEAD + TAIL
NODES = 8
NT = (((1,), (1,)), ((), ()))
TN = (((0,), (0,)), ((), ()))


def dot(left, right, dims=(((1,), (0,)), ((), ()))):
    return lax.dot_general(left, right, dims, preferred_element_type=F32)


def columns_of(routes, experts):
    tokens = routes.shape[0]
    lane = lax.broadcasted_iota(jnp.int32, (tokens, experts), 1)
    named = [routes[:, k : k + 1] == lane for k in range(2)]
    both = jnp.where(named[0] | named[1], 1.0, 0.0).astype(BF)
    before = lax.broadcasted_iota(jnp.int32, (tokens, tokens), 0) > lax.broadcasted_iota(
        jnp.int32, (tokens, tokens), 1
    )
    count = dot(jnp.where(before, 1.0, 0.0).astype(BF), both)
    found = []
    for k in range(2):
        rank = jnp.sum(jnp.where(named[k], count, 0.0), axis=1, keepdims=True).astype(jnp.int32)
        expert = routes[:, k : k + 1]
        head = jnp.where(rank < HEAD, expert * HEAD + rank, -1)
        tail = jnp.where(rank >= HEAD, expert * TAIL + rank - HEAD, -1)
        found.append((head, tail))
    return found


def onehot(column, width):
    lane = lax.broadcasted_iota(jnp.int32, (column.shape[0], width), 1)
    return jnp.where(column == lane, 1.0, 0.0).astype(BF)


def peer_of(me, k, planes, lanes):
    return ((me // lanes + k // lanes) % planes) * lanes + (me % lanes + k % lanes) % lanes


def drain(ref, sem):
    pltpu.make_async_copy(ref, ref, sem).wait()


def kernel(
    experts, sections, tokf, tokb, rf, rb, gf, gb, wg_h, wu_h, wd_h, sg_h, su_h, outf, outb,
    wg, wu, wd, sg, su, sgp, sup, sa, sb, ra, rbuf, part, got, sums, hid, ca, cb, da, db, osend, orecv,
    load_sem, own_sem, disp_s, disp_r, ret_s, ret_r, red_s, red_r, gat_s, gat_r, sec_s, sec_r,
):
    me = lax.axis_index("dev")
    node = lax.axis_index("node")
    section = lax.axis_index("section")
    lanes = 4 if experts % 4 == 0 else 1
    planes = experts // lanes
    x = node % 4
    bit_y, bit_1 = node // 4, x // 2
    bit_0 = (x + x // 2) % 2
    partner = {
        0: (node // 4) * 4 + x + 1 - 2 * (x % 2),
        1: (node // 4) * 4 + 3 - x,
        2: (node + 4) % 8,
    }
    block = bit_y * 4 + bit_1 * 2 + bit_0

    barrier = pltpu.get_barrier_semaphore()

    def greet(k, carry):
        pl.semaphore_signal(
            barrier, inc=1, device_id={"dev": peer_of(me, k, planes, lanes)}, device_id_type=MESH
        )
        return carry

    lax.fori_loop(1, experts, greet, 0)
    for d in range(3):
        pl.semaphore_signal(barrier, inc=1, device_id={"node": partner[d]}, device_id_type=MESH)
    pl.semaphore_signal(barrier, inc=1, device_id={"section": 1 - section}, device_id_type=MESH)

    share = pl.ds(pl.multiple_of(block * 128, 128), 128)
    loads = [
        pltpu.make_async_copy(wg_h, wg, load_sem.at[0]),
        pltpu.make_async_copy(wu_h, wu, load_sem.at[1]),
        pltpu.make_async_copy(wd_h, wd, load_sem.at[2]),
        pltpu.make_async_copy(sg_h.at[:, share], sg, load_sem.at[3]),
        pltpu.make_async_copy(su_h.at[:, share], su, load_sem.at[4]),
    ]
    for load in loads:
        load.start()

    for m, (tok, routes) in enumerate(((tokf, rf), (tokb, rb))):
        (h0, t0), (h1, t1) = columns_of(routes[...], experts)
        pick_head = onehot(h0, experts * HEAD) + onehot(h1, experts * HEAD)
        pick_tail = onehot(t0, experts * TAIL) + onehot(t1, experts * TAIL)
        rows = tok[...]
        width = rows.shape[1]
        sa[m] = dot(pick_head, rows, TN).astype(BF).reshape(experts, HEAD, width)
        sb[m] = dot(pick_tail, rows, TN).astype(BF).reshape(experts, TAIL, width)

    pl.semaphore_wait(barrier, experts - 1 + 4)

    def exchange(src_a, src_b, dst_a, dst_b, send, recv, m):
        def go(k, carry):
            p = peer_of(me, k, planes, lanes)
            for i, (src, dst) in enumerate(((src_a, dst_a), (src_b, dst_b))):
                pltpu.make_async_remote_copy(
                    src_ref=src.at[m, p],
                    dst_ref=dst.at[m, me],
                    send_sem=send.at[m, i],
                    recv_sem=recv.at[m, i],
                    device_id={"dev": p},
                    device_id_type=MESH,
                ).start()
            return carry

        lax.fori_loop(1, experts, go, 0)

    def keep(src_a, src_b, dst_a, dst_b, m):
        own = [
            pltpu.make_async_copy(src_a.at[m, me], dst_a.at[m, me], own_sem.at[0]),
            pltpu.make_async_copy(src_b.at[m, me], dst_b.at[m, me], own_sem.at[1]),
        ]
        for c in own:
            c.start()
        for c in own:
            c.wait()

    def settle(dst_a, dst_b, sems, m):
        drain(dst_a.at[m, pl.ds(0, experts - 1)], sems.at[m, 0])
        drain(dst_b.at[m, pl.ds(0, experts - 1)], sems.at[m, 1])

    exchange(sa, sb, ra, rbuf, disp_s, disp_r, 0)
    exchange(sa, sb, ra, rbuf, disp_s, disp_r, 1)
    keep(sa, sb, ra, rbuf, 0)
    keep(sa, sb, ra, rbuf, 1)

    for load in loads:
        load.wait()
    slots = experts * CAPACITY
    new = lax.broadcasted_iota(jnp.int32, (slots, 1), 0)
    late = new - experts * HEAD
    old = jnp.where(
        new < experts * HEAD,
        (new // HEAD) * CAPACITY + new % HEAD,
        (late // TAIL) * CAPACITY + HEAD + late % TAIL,
    )
    order = onehot(old, slots)
    sgp[...] = dot(order, sg[...])
    sup[...] = dot(order, su[...])

    half = slots // 2
    span = [pl.ds(0, half), pl.ds(half, half)]
    bits = {0: bit_0, 1: bit_1, 2: bit_y}

    def at(c, y, second, first):
        return y * 4 + (second * 2 + first if c == 0 else first * 2 + second)

    def axes(c):
        return (0, 1) if c == 0 else (1, 0)

    def remote(src, dst, send, recv, to):
        return pltpu.make_async_remote_copy(
            src_ref=src, dst_ref=dst, send_sem=send, recv_sem=recv,
            device_id={"node": partner[to]}, device_id_type=MESH,
        )

    def arrived_rows(a, b, m):
        return jnp.concatenate(
            [
                a[m].reshape(experts * HEAD, a.shape[-1]),
                b[m].reshape(experts * TAIL, b.shape[-1]),
            ],
            axis=0,
        )

    def partial(t, m, w, transposed):
        rows = arrived_rows(ra, rbuf, m)
        for j in range(4):
            if transposed:
                y = dot(rows, w[j * 256 : (j + 1) * 256, :], NT)
            else:
                y = dot(rows, w[:, j * 256 : (j + 1) * 256])
            y = y.astype(BF)
            part[t, 2 * j] = y[:, :128]
            part[t, 2 * j + 1] = y[:, 128:]

    def red_copy(t, c, i):
        d1, d2 = axes(c)
        n1, n2, ny = 1 - bits[d1], bits[d2], bits[2]
        if i < 4:
            second = 1 - n2 if i < 2 else n2
            y = 1 - ny if i % 2 == 0 else ny
            src, to = part.at[t, at(c, y, second, n1), span[c]], d1
        else:
            src, to = sums.at[t, c, i - 4], (d2 if i < 6 else 2)
        return remote(src, got.at[t, c, i], red_s.at[t, c, i], red_r.at[t, c, i], to)

    def mine(t, c, y, second):
        d1, _ = axes(c)
        return part[t, at(c, y, second, bits[d1]), span[c]].astype(F32)

    def red_start(t):
        for i in range(4):
            for c in range(2):
                red_copy(t, c, i).start()

    def red_a(t, i):
        for c in range(2):
            _, d2 = axes(c)
            red_copy(t, c, i).wait_recv()
            y = 1 - bits[2] if i == 0 else bits[2]
            value = mine(t, c, y, 1 - bits[d2]) + got[t, c, i].astype(F32)
            sums[t, c, i] = value.astype(BF)
            red_copy(t, c, 4 + i).start()

    def red_c(t):
        for c in range(2):
            _, d2 = axes(c)
            red_copy(t, c, 2).wait_recv()
            red_copy(t, c, 4).wait_recv()
            value = mine(t, c, 1 - bits[2], bits[d2]) + got[t, c, 2].astype(F32)
            sums[t, c, 2] = (value + got[t, c, 4].astype(F32)).astype(BF)
            red_copy(t, c, 6).start()

    def red_d(t, c):
        _, d2 = axes(c)
        for i in (3, 5, 6):
            red_copy(t, c, i).wait_recv()
        value = mine(t, c, bits[2], bits[d2]) + got[t, c, 3].astype(F32)
        return value + got[t, c, 5].astype(F32) + got[t, c, 6].astype(F32)

    def gat_copy(t, c, i):
        d1, d2 = axes(c)
        b1, b2, by = bits[d1], bits[d2], bits[2]
        y, second, to = (
            (by, b2, 2), (by, b2, d2), (1 - by, b2, d2),
            (by, b2, d1), (1 - by, b2, d1), (by, 1 - b2, d1), (1 - by, 1 - b2, d1),
        )[i]
        ref = hid.at[t, at(c, y, second, b1), span[c]]
        return remote(ref, ref, gat_s.at[t, c, i], gat_r.at[t, c, i], to)

    def gat_start(t, c):
        for i in (0, 1, 3):
            gat_copy(t, c, i).start()

    def gat_step(t, c, wait, starts):
        gat_copy(t, c, wait).wait_recv()
        for i in starts:
            gat_copy(t, c, i).start()

    def gat_middle(t):
        for wait, starts in ((0, (2, 4)), (1, (5,)), (2, (6,))):
            for c in range(2):
                gat_step(t, c, wait, starts)

    def gat_end(t):
        for c in range(2):
            for i in range(3, 7):
                gat_copy(t, c, i).wait_recv()

    def gathered(t):
        return jnp.concatenate([hid[t, b] for b in range(NODES)], axis=1)

    def send_back(m, value):
        value = value.astype(BF)
        cut = experts * HEAD
        ca[m] = value[:cut].reshape(experts, HEAD, value.shape[1])
        cb[m] = value[cut:].reshape(experts, TAIL, value.shape[1])
        exchange(ca, cb, da, db, ret_s, ret_r, m)
        keep(ca, cb, da, db, m)

    settle(ra, rbuf, disp_r, 0)
    partial(0, 0, wg, False)
    red_start(0)
    partial(1, 0, wu, False)
    red_start(1)
    for t in (0, 1):
        red_a(t, 0)
        red_a(t, 1)
    settle(ra, rbuf, disp_r, 1)
    partial(2, 1, wd, True)
    red_start(2)
    for t in (0, 1):
        red_c(t)
    for c in range(2):
        gate, up = red_d(0, c), red_d(1, c)
        hid[0, block, span[c]] = (jax.nn.silu(gate) * up).astype(BF)
        gat_start(0, c)
    red_a(2, 0)
    red_a(2, 1)
    gat_middle(0)
    red_c(2)
    for c in range(2):
        grad = red_d(2, c)
        a, u = sgp[span[c]], sup[span[c]]
        q = jax.nn.sigmoid(a)
        hid[1, block, span[c]] = (grad * u * q * (1.0 + a * (1.0 - q))).astype(BF)
        hid[2, block, span[c]] = (grad * a * q).astype(BF)
        gat_start(1, c)
        gat_start(2, c)
    gat_end(0)
    send_back(0, dot(gathered(0), wd[...]))
    gat_middle(1)
    gat_middle(2)
    gat_end(1)
    gat_end(2)
    send_back(1, dot(gathered(1), wg[...], NT) + dot(gathered(2), wu[...], NT))

    final = []
    for m, (tok, routes, gates, out) in enumerate(((tokf, rf, gf, outf), (tokb, rb, gb, outb))):
        settle(da, db, ret_r, m)
        heads, tails = arrived_rows(da, db, m)[: experts * HEAD], arrived_rows(da, db, m)[experts * HEAD :]
        mixed = tok[...].astype(F32)
        weighted = None
        for k, (head, tail) in enumerate(columns_of(routes[...], experts)):
            picked = dot(onehot(head, experts * HEAD), heads) + dot(onehot(tail, experts * TAIL), tails)
            term = gates[:, k : k + 1] * picked
            weighted = term if weighted is None else weighted + term
        osend[m] = (mixed + weighted).astype(BF)
        copy = pltpu.make_async_remote_copy(
            src_ref=osend.at[m], dst_ref=orecv.at[m], send_sem=sec_s.at[m], recv_sem=sec_r.at[m],
            device_id={"section": 1 - section}, device_id_type=MESH,
        )
        copy.start()
        final.append((copy, out))
    for m, (copy, out) in enumerate(final):
        copy.wait_recv()
        out[...] = orecv[m]

    for m in range(2):
        settle(sa, sb, disp_s, m)
        settle(ca, cb, ret_s, m)
        final[m][0].wait_send()
    for t in range(3):
        for c in range(2):
            for i in range(7):
                red_copy(t, c, i).wait_send()
                gat_copy(t, c, i).wait_send()


def solution(mesh):
    experts, sections = mesh.shape["dev"], mesh.shape["section"]

    def shards(inf, rf, gf, inb, rb, gb, wg, wu, wd, sg, su):
        args = [v[0] for v in (inf, inb, rf, rb, gf, gb)] + [v[0, 0] for v in (wg, wu, wd, sg, su)]
        tokens, width = args[0].shape
        slots, hidden = args[9].shape
        half, share = slots // 2, hidden // NODES
        vm = lambda *shape: pltpu.VMEM(shape, BF)
        both = [vm(2, experts, HEAD, width), vm(2, experts, TAIL, width)]
        dma = pltpu.SemaphoreType.DMA
        outs = pl.pallas_call(
            functools.partial(kernel, experts, sections),
            out_shape=[jax.ShapeDtypeStruct((tokens, width), BF)] * 2,
            in_specs=[pl.BlockSpec(memory_space=pltpu.VMEM)] * 6 + [pl.BlockSpec(memory_space=pl.ANY)] * 5,
            out_specs=[pl.BlockSpec(memory_space=pltpu.VMEM)] * 2,
            scratch_shapes=[vm(width, hidden), vm(width, hidden), vm(hidden, width), vm(slots, share), vm(slots, share)]
            + [pltpu.VMEM((slots, share), F32)] * 2
            + both + both
            + [vm(3, NODES, slots, share), vm(3, 2, 7, half, share), vm(3, 2, 3, half, share), vm(3, NODES, slots, share)]
            + both + both
            + [vm(2, tokens, width)] * 2
            + [dma((5,)), dma((2,))] + [dma((2, 2))] * 4 + [dma((3, 2, 7))] * 4 + [dma((2,))] * 2,
            compiler_params=pltpu.CompilerParams(
                collective_id=0, has_side_effects=True, vmem_limit_bytes=56 * 1024 * 1024
            ),
            name="relay_layer",
        )(*args)
        return tuple(o[None] for o in outs)

    return jax.shard_map(
        shards,
        mesh=mesh,
        in_specs=(P("section", "dev", "node"), P("section", "dev", None), P("section", "dev", None)) * 2
        + (P("section", "dev", "node", None),) * 2
        + (P("section", "dev", None, "node"),)
        + (P("section", "dev", None, None),) * 2,
        out_specs=(P("section", "dev", "node"), P("section", "dev", "node")),
        check_vma=False,
    )
```

```python
import functools

import jax
import jax.numpy as jnp
from jax import lax
from jax.experimental import pallas as pl
from jax.experimental.pallas import tpu as pltpu
from jax.sharding import PartitionSpec as P

MESH = pl.DeviceIdType.MESH
BF, F32 = jnp.bfloat16, jnp.float32
HEAD, TAIL = 8, 2
CAPACITY = HEAD + TAIL
NODES = 8
LANES = 4
GROUPS = ((0, 1, 11), (2, 10, 3), (6, 5, 7), (4, 8, 9))
PLANES = 12
CHUNKS = len(GROUPS)
DISTANCE = tuple(d for group in GROUPS for d in group)
NN = (((1,), (0,)), ((), ()))
NT = (((1,), (1,)), ((), ()))
TN = (((0,), (0,)), ((), ()))
PAD = 64


def dot(left, right, dims=NN):
    return lax.dot_general(left, right, dims, preferred_element_type=F32)


def table(index, values):
    found = jnp.zeros_like(index)
    for i, value in enumerate(values):
        found = jnp.where(index == i, value, found)
    return found


def iota(shape, dim):
    return lax.broadcasted_iota(jnp.int32, shape, dim)


def drain(ref, sem):
    pltpu.make_async_copy(ref, ref, sem).wait()


def widen(first, second):
    return jnp.concatenate(
        [first[:, :384], first[:, 384:] + second[:, :128], second[:, 128:]], axis=1
    ).astype(BF)


def kernel(
    experts, tokf, tokb, rf, rb, gf, gb, wg_h, wu_h, wd_h, sg_h, su_h, outf, outb,
    wg, wu, wd, sg, su, for_gate, for_up, sel, sa, sb, ra, rb_in, part, got, sums, hid, ca, cb, da, db, acc, osend, orecv,
    load_sem, own_sem, disp_s, disp_r, ret_s, ret_r, red_s, red_r, gat_s, gat_r, sec_s, sec_r,
):
    me = lax.axis_index("dev")
    node = lax.axis_index("node")
    section = lax.axis_index("section")
    z, lane = me // LANES, me % LANES
    x = node % 4
    bits = {0: (x + x // 2) % 2, 1: x // 2, 2: node // 4}
    partner = {
        0: (node // 4) * 4 + x + 1 - 2 * (x % 2),
        1: (node // 4) * 4 + 3 - x,
        2: (node + 4) % 8,
    }
    block = bits[2] * 4 + bits[1] * 2 + bits[0]
    group = experts // CHUNKS
    slots = experts * CAPACITY
    rows = slots // CHUNKS
    cut = group * HEAD

    def ahead(dz, dy):
        return ((z + dz) % PLANES) * LANES + (lane + dy) % LANES

    def behind(dz, dy):
        return ((z + PLANES - dz) % PLANES) * LANES + (lane + LANES - dy) % LANES

    barrier = pltpu.get_barrier_semaphore()

    def greet(k, carry):
        pl.semaphore_signal(
            barrier, inc=1, device_id={"dev": (me + k) % experts}, device_id_type=MESH
        )
        return carry

    lax.fori_loop(1, experts, greet, 0)
    for d in range(3):
        pl.semaphore_signal(barrier, inc=1, device_id={"node": partner[d]}, device_id_type=MESH)
    pl.semaphore_signal(barrier, inc=1, device_id={"section": 1 - section}, device_id_type=MESH)

    inner = pl.ds(PAD, wg_h.shape[0])
    for w in (wg, wu, wd):
        w[:PAD] = jnp.zeros((PAD, w.shape[1]), BF)
        w[w.shape[0] - PAD :] = jnp.zeros((PAD, w.shape[1]), BF)
    loads = [
        pltpu.make_async_copy(wg_h, wg.at[inner], load_sem.at[0]),
        pltpu.make_async_copy(wu_h, wu.at[inner], load_sem.at[1]),
        pltpu.make_async_copy(wd_h, wd.at[inner], load_sem.at[2]),
        pltpu.make_async_copy(sg_h, sg, load_sem.at[3]),
        pltpu.make_async_copy(su_h, su, load_sem.at[4]),
    ]
    for load in loads:
        load.start()
    front, back = pl.ds(0, 512), pl.ds(PAD, 512)

    tokens = rf.shape[1]
    for m, routes in enumerate((rf, rb)):
        named = [routes[k : k + 1, :] == iota((experts, tokens), 0) for k in range(2)]
        both = jnp.where(named[0] | named[1], 1.0, 0.0).astype(BF)
        earlier = jnp.where(iota((tokens, tokens), 0) < iota((tokens, tokens), 1), 1.0, 0.0)
        count = dot(both, earlier.astype(BF))
        for k in range(2):
            rank = jnp.sum(jnp.where(named[k], count, 0.0), axis=0, keepdims=True).astype(jnp.int32)
            expert = routes[k : k + 1, :]
            dz = (expert // LANES + PLANES - z) % PLANES
            dy = (expert % LANES + LANES - lane) % LANES
            place = table(dz, [DISTANCE.index(d) for d in range(PLANES)]) * LANES + dy
            chunk, local = place // group, place % group
            slot = chunk * rows + jnp.where(
                rank < HEAD, local * HEAD + rank, cut + local * TAIL + rank - HEAD
            )
            sel[m, :, k * tokens : (k + 1) * tokens] = jnp.where(
                slot == iota((slots, tokens), 0), 1.0, 0.0
            ).astype(BF)

    gap = jnp.zeros((PAD, tokens), BF)
    wide = (
        jnp.concatenate([tokf[...], gap], axis=0),
        jnp.concatenate([gap, tokb[...]], axis=0),
    )

    def split(value, head, tail, c):
        width = value.shape[1]
        ks = slice(c * group, (c + 1) * group)
        head[ks] = value[:cut].reshape(group, HEAD, width)
        tail[ks] = value[cut:].reshape(group, TAIL, width)

    def joined(head, tail, c):
        ks = slice(c * group, (c + 1) * group)
        width = head.shape[-1]
        return jnp.concatenate(
            [head[ks].reshape(cut, width), tail[ks].reshape(group * TAIL, width)], axis=0
        )

    def pack(c):
        halves = []
        for m in range(2):
            chosen = sel[m, c * rows : (c + 1) * rows, :]
            halves.append(dot(chosen[:, :tokens] + chosen[:, tokens:], wide[m], NT))
        split(widen(*halves), sa, sb, c)

    def exchange(c, pairs, send, recv, to):
        for i, dz in enumerate(GROUPS[c]):
            first = (c * len(GROUPS[c]) + i) * LANES

            def go(dy, carry, first=first, dz=dz):
                for j, (src, dst) in enumerate(pairs):
                    pltpu.make_async_remote_copy(
                        src_ref=src.at[first + dy],
                        dst_ref=dst.at[first + dy],
                        send_sem=send.at[j],
                        recv_sem=recv.at[c, j],
                        device_id={"dev": to(dz, dy)},
                        device_id_type=MESH,
                    ).start()
                return carry

            lax.fori_loop(1 if dz == 0 else 0, LANES, go, 0)
            if dz == 0:
                own = [
                    pltpu.make_async_copy(src.at[first], dst.at[first], own_sem.at[j])
                    for j, (src, dst) in enumerate(pairs)
                ]
                for copy in own:
                    copy.start()
                for copy in own:
                    copy.wait()

    def settle(c, pairs, recv):
        for j, (_, dst) in enumerate(pairs):
            drain(dst.at[pl.ds(0, group - (0 in GROUPS[c]))], recv.at[c, j])

    out_pairs = ((sa, ra), (sb, rb_in))
    back_pairs = ((ca, da), (cb, db))

    for c in range(CHUNKS):
        pack(c)
        if c == 0:
            pl.semaphore_wait(barrier, experts - 1 + 4)
        exchange(c, out_pairs, disp_s, disp_r, ahead)

    for load in loads[:3]:
        load.wait()

    def factors():
        for load in loads[3:]:
            load.wait()
        new = iota((slots, 1), 0)
        chunk, local = new // rows, new % rows
        late = local - cut
        place = chunk * group + jnp.where(local < cut, local // HEAD, late // TAIL)
        rank = jnp.where(local < cut, local % HEAD, HEAD + late % TAIL)
        dz, dy = table(place // LANES, DISTANCE), place % LANES
        old = behind(dz, dy) * CAPACITY + rank
        order = jnp.where(old == iota((slots, slots), 1), 1.0, 0.0).astype(BF)
        for j in range(4):
            span = slice(j * 256, (j + 1) * 256)
            a, u = dot(order, sg[:, span]), dot(order, su[:, span])
            q = jax.nn.sigmoid(a)
            for_gate[:, span] = u * q * (1.0 + a * (1.0 - q))
            for_up[:, span] = a * q

    def axes(t, c):
        return (0, 1) if (t + c) % 2 == 0 else (1, 0)

    def at(t, c, y, second, first):
        return y * 4 + (second * 2 + first if axes(t, c)[0] == 0 else first * 2 + second)

    def remote(src, dst, send, recv, to):
        return pltpu.make_async_remote_copy(
            src_ref=src, dst_ref=dst, send_sem=send, recv_sem=recv,
            device_id={"node": partner[to]}, device_id_type=MESH,
        )

    def red_copy(t, c, i):
        d1, d2 = axes(t, c)
        n1, n2, ny = 1 - bits[d1], bits[d2], bits[2]
        if i < 4:
            second = 1 - n2 if i < 2 else n2
            y = 1 - ny if i % 2 == 0 else ny
            src, to = part.at[t, c, at(t, c, y, second, n1)], d1
        else:
            src, to = sums.at[t, c, i - 4], (d2 if i < 6 else 2)
        return remote(src, got.at[t, c, i], red_s.at[t, c, i], red_r.at[t, c, i], to)

    def mine(t, c, y, second):
        d1, _ = axes(t, c)
        return part[t, c, at(t, c, y, second, bits[d1])].astype(F32)

    def red_start(t, c):
        for i in range(4):
            red_copy(t, c, i).start()

    def red_a(t, c, i):
        _, d2 = axes(t, c)
        red_copy(t, c, i).wait_recv()
        y = 1 - bits[2] if i == 0 else bits[2]
        value = mine(t, c, y, 1 - bits[d2]) + got[t, c, i].astype(F32)
        sums[t, c, i] = value.astype(BF)
        red_copy(t, c, 4 + i).start()

    def red_c(t, c):
        _, d2 = axes(t, c)
        red_copy(t, c, 2).wait_recv()
        red_copy(t, c, 4).wait_recv()
        value = mine(t, c, 1 - bits[2], bits[d2]) + got[t, c, 2].astype(F32)
        sums[t, c, 2] = (value + got[t, c, 4].astype(F32)).astype(BF)
        red_copy(t, c, 6).start()

    def red_d(t, c):
        _, d2 = axes(t, c)
        for i in (3, 5, 6):
            red_copy(t, c, i).wait_recv()
        value = mine(t, c, bits[2], bits[d2]) + got[t, c, 3].astype(F32)
        return value + got[t, c, 5].astype(F32) + got[t, c, 6].astype(F32)

    def gat_copy(t, c, i):
        d1, d2 = axes(t, c)
        b1, b2, by = bits[d1], bits[d2], bits[2]
        y, second, to = (
            (by, b2, 2), (by, b2, d2), (1 - by, b2, d2),
            (by, b2, d1), (1 - by, b2, d1), (by, 1 - b2, d1), (1 - by, 1 - b2, d1),
        )[i]
        ref = hid.at[t, c, at(t, c, y, second, b1)]
        return remote(ref, ref, gat_s.at[t, c, i], gat_r.at[t, c, i], to)

    def gat_start(t, c):
        for i in (0, 1, 3):
            gat_copy(t, c, i).start()

    def gathered(t, c):
        return jnp.concatenate([hid[t, c, b] for b in range(NODES)], axis=1)

    def products(c):
        settle(c, out_pairs, disp_r)
        arrived = joined(ra, rb_in, c)
        for t, (value, w, zone) in enumerate(
            ((arrived[:, :512], wg, back), (arrived[:, :512], wu, back), (arrived[:, 384:], wd, front))
        ):
            for j in range(4):
                y = dot(value, w[zone, j * 256 : (j + 1) * 256]).astype(BF)
                part[t, c, 2 * j] = y[:, :128]
                part[t, c, 2 * j + 1] = y[:, 128:]
            red_start(t, c)

    def halve(c):
        for i in range(2):
            for t in range(3):
                red_a(t, c, i)

    def settle_y(c):
        for t in range(3):
            red_c(t, c)

    def activate(c):
        gate, up = red_d(0, c), red_d(1, c)
        hid[0, c, block] = (jax.nn.silu(gate) * up).astype(BF)
        gat_start(0, c)
        hid[1, c, block] = red_d(2, c).astype(BF)
        gat_start(1, c)

    def forward(c):
        for wait, starts in ((0, (2, 4)), (1, (5,)), (2, (6,))):
            for t in range(2):
                gat_copy(t, c, wait).wait_recv()
                for i in starts:
                    gat_copy(t, c, i).start()

    def finish(c):
        for t in range(2):
            for i in range(3, 7):
                gat_copy(t, c, i).wait_recv()
        first = dot(gathered(0, c), wd[back, :], NT)
        grad = gathered(1, c).astype(F32)
        mine_rows = slice(c * rows, (c + 1) * rows)
        second = dot((grad * for_gate[mine_rows, :]).astype(BF), wg[front, :], NT)
        second = second + dot((grad * for_up[mine_rows, :]).astype(BF), wu[front, :], NT)
        split(widen(first, second), ca, cb, c)
        exchange(c, back_pairs, ret_s, ret_r, behind)

    stages = {"W": products, "A": halve, "C": settle_y, "D": activate, "G": forward, "E": finish, "F": lambda _: factors()}
    for step in ORDER:
        stages[step[0]](int(step[1]))

    for c in range(CHUNKS):
        settle(c, back_pairs, ret_r)
        returned = joined(da, db, c)
        for m in range(2):
            value = returned[:, :512] if m == 0 else returned[:, 384:]
            picked = dot(value, sel[m, c * rows : (c + 1) * rows, :], TN)
            acc[m] = picked if c == 0 else acc[m] + picked
    final = []
    for m, (tok, gates, out) in enumerate(((tokf, gf, outf), (tokb, gb, outb))):
        picked = acc[m, : 512 - PAD, :] if m == 0 else acc[m, PAD:, :]
        weighted = gates[0:1, :] * picked[:, :tokens] + gates[1:2, :] * picked[:, tokens:]
        osend[m] = (tok[...].astype(F32) + weighted).astype(BF)
        copy = pltpu.make_async_remote_copy(
            src_ref=osend.at[m], dst_ref=orecv.at[m], send_sem=sec_s.at[m], recv_sem=sec_r.at[m],
            device_id={"section": 1 - section}, device_id_type=MESH,
        )
        copy.start()
        final.append((copy, out))
    for m, (copy, out) in enumerate(final):
        copy.wait_recv()
        out[...] = orecv[m]

    for pairs, sems in ((out_pairs, disp_s), (back_pairs, ret_s)):
        for j, (src, _) in enumerate(pairs):
            drain(src.at[pl.ds(0, experts - 1)], sems.at[j])
    for copy, _ in final:
        copy.wait_send()
    for t in range(3):
        for c in range(CHUNKS):
            for i in range(7):
                red_copy(t, c, i).wait_send()
                if t < 2:
                    gat_copy(t, c, i).wait_send()


ORDER = ("W0", "F0", "A0", "C0", "D0", "W1", "G0", "A1", "E0", "C1", "W2", "D1", "A2", "G1", "C2", "W3", "E1", "D2", "A3", "G2", "C3", "E2", "D3", "G3", "E3")


def solution(mesh):
    experts = mesh.shape["dev"]

    def shards(inf, rf, gf, inb, rb, gb, wg, wu, wd, sg, su):
        args = [v[0].T for v in (inf, inb, rf, rb, gf, gb)]
        args += [wg[0, 0], wu[0, 0], wd[0, 0].T, sg[0, 0], su[0, 0]]
        width, tokens = args[0].shape
        slots, hidden = args[9].shape
        rows, share = slots // CHUNKS, hidden // NODES
        vm = lambda *shape: pltpu.VMEM(shape, BF)
        both = [vm(experts, HEAD, 2 * width), vm(experts, TAIL, 2 * width)]
        dma = pltpu.SemaphoreType.DMA
        outs = pl.pallas_call(
            functools.partial(kernel, experts),
            out_shape=[jax.ShapeDtypeStruct((width, tokens), BF)] * 2,
            in_specs=[pl.BlockSpec(memory_space=pltpu.VMEM)] * 6 + [pl.BlockSpec(memory_space=pl.ANY)] * 5,
            out_specs=[pl.BlockSpec(memory_space=pltpu.VMEM)] * 2,
            scratch_shapes=[vm(width + 2 * PAD, hidden)] * 3
            + [vm(slots, hidden)] * 2
            + [pltpu.VMEM((slots, hidden), F32)] * 2
            + [vm(2, slots, 2 * tokens)]
            + both + both
            + [vm(3, CHUNKS, NODES, rows, share), vm(3, CHUNKS, 7, rows, share)]
            + [vm(3, CHUNKS, 3, rows, share), vm(2, CHUNKS, NODES, rows, share)]
            + both + both
            + [pltpu.VMEM((2, width + PAD, 2 * tokens), F32)]
            + [vm(2, width, tokens)] * 2
            + [dma((5,)), dma((2,)), dma((2,)), dma((CHUNKS, 2)), dma((2,)), dma((CHUNKS, 2))]
            + [dma((3, CHUNKS, 7))] * 2 + [dma((2, CHUNKS, 7))] * 2 + [dma((2,))] * 2,
            compiler_params=pltpu.CompilerParams(
                collective_id=0, has_side_effects=True, vmem_limit_bytes=56 * 1024 * 1024
            ),
            name="relay_layer",
        )(*args)
        return tuple(o.T[None] for o in outs)

    return jax.shard_map(
        shards,
        mesh=mesh,
        in_specs=(P("section", "dev", "node"), P("section", "dev", None), P("section", "dev", None)) * 2
        + (P("section", "dev", "node", None),) * 2
        + (P("section", "dev", None, "node"),)
        + (P("section", "dev", None, None),) * 2,
        out_specs=(P("section", "dev", "node"), P("section", "dev", "node")),
        check_vma=False,
    )
```

```python
import functools

import jax
import jax.numpy as jnp
from jax import lax
from jax.experimental import pallas as pl
from jax.experimental.pallas import tpu as pltpu
from jax.sharding import PartitionSpec as P

MESH = pl.DeviceIdType.MESH
BF, F32 = jnp.bfloat16, jnp.float32
HEAD, TAIL = 8, 2
CAPACITY = HEAD + TAIL
NODES = 8
LANES = 4
GROUPS = ((0, 1, 11), (4, 8, 9), (6, 5, 7), (2, 10, 3))
PLANES = 12
CHUNKS = len(GROUPS)
DISTANCE = tuple(d for group in GROUPS for d in group)
NN = (((1,), (0,)), ((), ()))
NT = (((1,), (1,)), ((), ()))
TN = (((0,), (0,)), ((), ()))
PAD = 64


def dot(left, right, dims=NN):
    return lax.dot_general(left, right, dims, preferred_element_type=F32)


def table(index, values):
    found = jnp.zeros_like(index)
    for i, value in enumerate(values):
        found = jnp.where(index == i, value, found)
    return found


def iota(shape, dim):
    return lax.broadcasted_iota(jnp.int32, shape, dim)


def drain(ref, sem):
    pltpu.make_async_copy(ref, ref, sem).wait()


def widen(first, second):
    return jnp.concatenate(
        [first[:, :384], first[:, 384:] + second[:, :128], second[:, 128:]], axis=1
    ).astype(BF)


def kernel(
    experts, tokf, tokb, rf, rb, gf, gb, wg_h, wu_h, wd_h, sg_h, su_h, outf, outb,
    wg, wu, wd, sg, su, for_gate, for_up, sel, sa, sb, ra, rb_in, part, got, sums, hid, ca, cb, da, db, acc, osel, otokf, otokb, ogf, ogb,
    load_sem, own_sem, disp_s, disp_r, ret_s, ret_r, red_s, red_r, gat_s, gat_r, sec_s, sec_r,
):
    me = lax.axis_index("dev")
    node = lax.axis_index("node")
    section = lax.axis_index("section")
    z, lane = me // LANES, me % LANES
    x = node % 4
    bits = {0: (x + x // 2) % 2, 1: x // 2, 2: node // 4}
    partner = {
        0: (node // 4) * 4 + x + 1 - 2 * (x % 2),
        1: (node // 4) * 4 + 3 - x,
        2: (node + 4) % 8,
    }
    block = bits[2] * 4 + bits[1] * 2 + bits[0]
    group = experts // CHUNKS
    slots = experts * CAPACITY
    rows = slots // CHUNKS
    cut = group * HEAD

    def ahead(dz, dy):
        return ((z + dz) % PLANES) * LANES + (lane + dy) % LANES

    def behind(dz, dy):
        return ((z + PLANES - dz) % PLANES) * LANES + (lane + LANES - dy) % LANES

    barrier = pltpu.get_barrier_semaphore()

    def greet(k, carry):
        pl.semaphore_signal(
            barrier, inc=1, device_id={"dev": (me + k) % experts}, device_id_type=MESH
        )
        pl.semaphore_signal(
            barrier, inc=1, device_id={"dev": (me + k) % experts, "section": 1 - section},
            device_id_type=MESH,
        )
        return carry

    lax.fori_loop(1, experts, greet, 0)
    for d in range(3):
        pl.semaphore_signal(barrier, inc=1, device_id={"node": partner[d]}, device_id_type=MESH)
    pl.semaphore_signal(barrier, inc=1, device_id={"section": 1 - section}, device_id_type=MESH)

    inner = pl.ds(PAD, wg_h.shape[0])
    for w in (wg, wu, wd):
        w[:PAD] = jnp.zeros((PAD, w.shape[1]), BF)
        w[w.shape[0] - PAD :] = jnp.zeros((PAD, w.shape[1]), BF)
    loads = [
        pltpu.make_async_copy(wg_h, wg.at[inner], load_sem.at[0]),
        pltpu.make_async_copy(wu_h, wu.at[inner], load_sem.at[1]),
        pltpu.make_async_copy(wd_h, wd.at[inner], load_sem.at[2]),
        pltpu.make_async_copy(sg_h, sg, load_sem.at[3]),
        pltpu.make_async_copy(su_h, su, load_sem.at[4]),
    ]
    for load in loads:
        load.start()
    front, back = pl.ds(0, 512), pl.ds(PAD, 512)

    tokens = rf.shape[1]
    for m, routes in enumerate((rf, rb)):
        named = [routes[k : k + 1, :] == iota((experts, tokens), 0) for k in range(2)]
        both = jnp.where(named[0] | named[1], 1.0, 0.0).astype(BF)
        earlier = jnp.where(iota((tokens, tokens), 0) < iota((tokens, tokens), 1), 1.0, 0.0)
        count = dot(both, earlier.astype(BF))
        for k in range(2):
            rank = jnp.sum(jnp.where(named[k], count, 0.0), axis=0, keepdims=True).astype(jnp.int32)
            expert = routes[k : k + 1, :]
            dz = (expert // LANES + PLANES - z) % PLANES
            dy = (expert % LANES + LANES - lane) % LANES
            place = table(dz, [DISTANCE.index(d) for d in range(PLANES)]) * LANES + dy
            chunk, local = place // group, place % group
            slot = chunk * rows + jnp.where(
                rank < HEAD, local * HEAD + rank, cut + local * TAIL + rank - HEAD
            )
            sel[m, :, k * tokens : (k + 1) * tokens] = jnp.where(
                slot == iota((slots, tokens), 0), 1.0, 0.0
            ).astype(BF)

    gap = jnp.zeros((PAD, tokens), BF)
    wide = (
        jnp.concatenate([tokf[...], gap], axis=0),
        jnp.concatenate([gap, tokb[...]], axis=0),
    )

    def split(value, head, tail, c):
        width = value.shape[1]
        ks = slice(c * group, (c + 1) * group)
        head[ks] = value[:cut].reshape(group, HEAD, width)
        tail[ks] = value[cut:].reshape(group, TAIL, width)

    def joined(head, tail, c):
        ks = slice(c * group, (c + 1) * group)
        width = head.shape[-1]
        return jnp.concatenate(
            [head[ks].reshape(cut, width), tail[ks].reshape(group * TAIL, width)], axis=0
        )

    def pack(c):
        halves = []
        for m in range(2):
            chosen = sel[m, c * rows : (c + 1) * rows, :]
            halves.append(dot(chosen[:, :tokens] + chosen[:, tokens:], wide[m], NT))
        split(widen(*halves), sa, sb, c)

    def exchange(c, pairs, send, recv, to, across):
        for i, dz in enumerate(GROUPS[c]):
            first = (c * len(GROUPS[c]) + i) * LANES

            def go(dy, carry, first=first, dz=dz):
                for j, (src, dst) in enumerate(pairs):
                    pltpu.make_async_remote_copy(
                        src_ref=src.at[first + dy],
                        dst_ref=dst.at[first + dy],
                        send_sem=send.at[j],
                        recv_sem=recv.at[c, j],
                        device_id={"dev": to(dz, dy), "section": 1 - section if across else section},
                        device_id_type=MESH,
                    ).start()
                return carry

            lax.fori_loop(1 if dz == 0 and not across else 0, LANES, go, 0)
            if dz == 0 and not across:
                own = [
                    pltpu.make_async_copy(src.at[first], dst.at[first], own_sem.at[j])
                    for j, (src, dst) in enumerate(pairs)
                ]
                for copy in own:
                    copy.start()
                for copy in own:
                    copy.wait()

    def settle(c, pairs, recv, across):
        for j, (_, dst) in enumerate(pairs):
            drain(dst.at[pl.ds(0, group - (0 in GROUPS[c] and not across))], recv.at[c, j])

    out_pairs = ((sa, ra), (sb, rb_in))
    back_pairs = ((ca, da), (cb, db))

    for c in range(CHUNKS):
        pack(c)
        if c == 0:
            pl.semaphore_wait(barrier, 2 * (experts - 1) + 4)
        exchange(c, out_pairs, disp_s, disp_r, ahead, False)
    handed = [
        pltpu.make_async_remote_copy(
            src_ref=src, dst_ref=dst, send_sem=sec_s.at[i], recv_sem=sec_r.at[i],
            device_id={"section": 1 - section}, device_id_type=MESH,
        )
        for i, (src, dst) in enumerate(
            ((sel, osel), (tokf, otokf), (tokb, otokb), (gf, ogf), (gb, ogb))
        )
    ]
    for copy in handed:
        copy.start()

    for load in loads[:3]:
        load.wait()

    def factors():
        for load in loads[3:]:
            load.wait()
        new = iota((slots, 1), 0)
        chunk, local = new // rows, new % rows
        late = local - cut
        place = chunk * group + jnp.where(local < cut, local // HEAD, late // TAIL)
        rank = jnp.where(local < cut, local % HEAD, HEAD + late % TAIL)
        dz, dy = table(place // LANES, DISTANCE), place % LANES
        old = behind(dz, dy) * CAPACITY + rank
        order = jnp.where(old == iota((slots, slots), 1), 1.0, 0.0).astype(BF)
        for j in range(4):
            span = slice(j * 256, (j + 1) * 256)
            a, u = dot(order, sg[:, span]), dot(order, su[:, span])
            q = jax.nn.sigmoid(a)
            for_gate[:, span] = u * q * (1.0 + a * (1.0 - q))
            for_up[:, span] = a * q

    def axes(t, c):
        return tuple("aby".index(axis) for axis in TRAVEL[c][t])

    def at(t, c, third, second, first):
        return sum(bit << d for bit, d in zip((first, second, third), axes(t, c)))

    def remote(src, dst, send, recv, to):
        return pltpu.make_async_remote_copy(
            src_ref=src, dst_ref=dst, send_sem=send, recv_sem=recv,
            device_id={"node": partner[to]}, device_id_type=MESH,
        )

    def red_copy(t, c, i):
        d1, d2, d3 = axes(t, c)
        n1, n2, ny = 1 - bits[d1], bits[d2], bits[d3]
        if i < 4:
            second = 1 - n2 if i < 2 else n2
            y = 1 - ny if i % 2 == 0 else ny
            src, to = part.at[t, c, at(t, c, y, second, n1)], d1
        else:
            src, to = sums.at[t, c, i - 4], (d2 if i < 6 else d3)
        return remote(src, got.at[t, c, i], red_s.at[t, c, i], red_r.at[t, c, i], to)

    def mine(t, c, y, second):
        d1, _, _ = axes(t, c)
        return part[t, c, at(t, c, y, second, bits[d1])].astype(F32)

    def red_start(t, c):
        for i in range(4):
            red_copy(t, c, i).start()

    def red_a(t, c, i):
        _, d2, d3 = axes(t, c)
        red_copy(t, c, i).wait_recv()
        y = 1 - bits[d3] if i == 0 else bits[d3]
        value = mine(t, c, y, 1 - bits[d2]) + got[t, c, i].astype(F32)
        sums[t, c, i] = value.astype(BF)
        red_copy(t, c, 4 + i).start()

    def red_c(t, c):
        _, d2, d3 = axes(t, c)
        red_copy(t, c, 2).wait_recv()
        red_copy(t, c, 4).wait_recv()
        value = mine(t, c, 1 - bits[d3], bits[d2]) + got[t, c, 2].astype(F32)
        sums[t, c, 2] = (value + got[t, c, 4].astype(F32)).astype(BF)
        red_copy(t, c, 6).start()

    def red_d(t, c):
        _, d2, d3 = axes(t, c)
        for i in (3, 5, 6):
            red_copy(t, c, i).wait_recv()
        value = mine(t, c, bits[d3], bits[d2]) + got[t, c, 3].astype(F32)
        return value + got[t, c, 5].astype(F32) + got[t, c, 6].astype(F32)

    def gat_copy(t, c, i):
        d1, d2, d3 = axes(t, c)
        b1, b2, by = bits[d1], bits[d2], bits[d3]
        y, second, to = (
            (by, b2, d3), (by, b2, d2), (1 - by, b2, d2),
            (by, b2, d1), (1 - by, b2, d1), (by, 1 - b2, d1), (1 - by, 1 - b2, d1),
        )[i]
        ref = hid.at[t, c, at(t, c, y, second, b1)]
        return remote(ref, ref, gat_s.at[t, c, i], gat_r.at[t, c, i], to)

    def gat_start(t, c):
        for i in (0, 1, 3):
            gat_copy(t, c, i).start()

    def gathered(t, c):
        return jnp.concatenate([hid[t, c, b] for b in range(NODES)], axis=1)

    def products(c):
        settle(c, out_pairs, disp_r, False)
        arrived = joined(ra, rb_in, c)
        for t, (value, w, zone) in enumerate(
            ((arrived[:, :512], wg, back), (arrived[:, :512], wu, back), (arrived[:, 384:], wd, front))
        ):
            for j in range(4):
                y = dot(value, w[zone, j * 256 : (j + 1) * 256]).astype(BF)
                part[t, c, 2 * j] = y[:, :128]
                part[t, c, 2 * j + 1] = y[:, 128:]
            red_start(t, c)

    def halve(c, i):
        for t in range(3):
            red_a(t, c, i)

    def settle_y(c):
        for t in range(3):
            red_c(t, c)

    def activate(c):
        gate, up = red_d(0, c), red_d(1, c)
        hid[0, c, block] = (jax.nn.silu(gate) * up).astype(BF)
        gat_start(0, c)
        hid[1, c, block] = red_d(2, c).astype(BF)
        gat_start(1, c)

    def forward(c, wait):
        for t in range(2):
            gat_copy(t, c, wait).wait_recv()
            for i in ((2, 4), (5,), (6,))[wait]:
                gat_copy(t, c, i).start()

    def finish(c):
        for t in range(2):
            for i in range(3, 7):
                gat_copy(t, c, i).wait_recv()
        first = dot(gathered(0, c), wd[back, :], NT)
        grad = gathered(1, c).astype(F32)
        mine_rows = slice(c * rows, (c + 1) * rows)
        second = dot((grad * for_gate[mine_rows, :]).astype(BF), wg[front, :], NT)
        second = second + dot((grad * for_up[mine_rows, :]).astype(BF), wu[front, :], NT)
        split(widen(first, second), ca, cb, c)
        exchange(c, back_pairs, ret_s, ret_r, behind, True)

    stages = {
        "F": lambda _: factors(),
        "W": products,
        "A": lambda c: halve(c, 0),
        "B": lambda c: halve(c, 1),
        "C": settle_y,
        "D": activate,
        "G": lambda c: forward(c, 0),
        "H": lambda c: forward(c, 1),
        "I": lambda c: forward(c, 2),
        "E": finish,
    }
    for step in ORDER:
        stages[step[0]](int(step[1]))

    for copy in handed:
        copy.wait_recv()
    for c in range(CHUNKS):
        settle(c, back_pairs, ret_r, True)
        returned = joined(da, db, c)
        for m in range(2):
            value = returned[:, :512] if m == 0 else returned[:, 384:]
            picked = dot(value, osel[m, c * rows : (c + 1) * rows, :], TN)
            acc[m] = picked if c == 0 else acc[m] + picked
    for m, (tok, gates, out) in enumerate(((otokf, ogf, outf), (otokb, ogb, outb))):
        picked = acc[m, : 512 - PAD, :] if m == 0 else acc[m, PAD:, :]
        weighted = gates[0:1, :] * picked[:, :tokens] + gates[1:2, :] * picked[:, tokens:]
        out[...] = (tok[...].astype(F32) + weighted).astype(BF)

    for pairs, sems, count in ((out_pairs, disp_s, experts - 1), (back_pairs, ret_s, experts)):
        for j, (src, _) in enumerate(pairs):
            drain(src.at[pl.ds(0, count)], sems.at[j])
    for copy in handed:
        copy.wait_send()
    for t in range(3):
        for c in range(CHUNKS):
            for i in range(7):
                red_copy(t, c, i).wait_send()
                if t < 2:
                    gat_copy(t, c, i).wait_send()


TRAVEL = (("aby", "bay", "aby"), ("bay", "aby", "bay"), ("aby", "bay", "aby"), ("bay", "aby", "bay"))
ORDER = ("W0", "F0", "A0", "B0", "C0", "D0", "W1", "A1", "B1", "G0", "H0", "C1", "I0", "D1", "W2", "G1", "A2", "H1", "B2", "E0", "I1", "W3", "C2", "D2", "E1", "G2", "A3", "H2", "I2", "B3", "C3", "E2", "D3", "G3", "H3", "I3", "E3")


def hand_over(first, second, first_out, second_out, first_buf, second_buf, sems):
    pairs = ((first, first_buf, first_out), (second, second_buf, second_out))
    into = [pltpu.make_async_copy(a, b, sems.at[i]) for i, (a, b, _) in enumerate(pairs)]
    away = [pltpu.make_async_copy(b, c, sems.at[2 + i]) for i, (_, b, c) in enumerate(pairs)]
    for copy in into:
        copy.start()
    for copy, onward in zip(into, away):
        copy.wait()
        onward.start()
    for copy in away:
        copy.wait()


def solution(mesh):
    experts = mesh.shape["dev"]

    def shards(inf, rf, gf, inb, rb, gb, wg, wu, wd, sg, su):
        args = [v[0].T for v in (inf, inb, rf, rb, gf, gb)]
        args += [wg[0, 0], wu[0, 0], wd[0, 0].T, sg[0, 0], su[0, 0]]
        width, tokens = args[0].shape
        slots, hidden = args[9].shape
        rows, share = slots // CHUNKS, hidden // NODES
        vm = lambda *shape: pltpu.VMEM(shape, BF)
        both = [vm(experts, HEAD, 2 * width), vm(experts, TAIL, 2 * width)]
        dma = pltpu.SemaphoreType.DMA
        outs = pl.pallas_call(
            functools.partial(kernel, experts),
            out_shape=[jax.ShapeDtypeStruct((width, tokens), BF)] * 2,
            in_specs=[pl.BlockSpec(memory_space=pltpu.VMEM)] * 6 + [pl.BlockSpec(memory_space=pl.ANY)] * 5,
            out_specs=[pl.BlockSpec(memory_space=pltpu.VMEM)] * 2,
            scratch_shapes=[vm(width + 2 * PAD, hidden)] * 3
            + [vm(slots, hidden)] * 2
            + [pltpu.VMEM((slots, hidden), F32)] * 2
            + [vm(2, slots, 2 * tokens)]
            + both + both
            + [vm(3, CHUNKS, NODES, rows, share), vm(3, CHUNKS, 7, rows, share)]
            + [vm(3, CHUNKS, 3, rows, share), vm(2, CHUNKS, NODES, rows, share)]
            + both + both
            + [pltpu.VMEM((2, width + PAD, 2 * tokens), F32)]
            + [vm(2, slots, 2 * tokens)] + [vm(width, tokens)] * 2 + [pltpu.VMEM((2, tokens), F32)] * 2
            + [dma((5,)), dma((2,)), dma((2,)), dma((CHUNKS, 2)), dma((2,)), dma((CHUNKS, 2))]
            + [dma((3, CHUNKS, 7))] * 2 + [dma((2, CHUNKS, 7))] * 2 + [dma((5,))] * 2,
            compiler_params=pltpu.CompilerParams(
                collective_id=0, has_side_effects=True, vmem_limit_bytes=56 * 1024 * 1024
            ),
            name="relay_layer",
        )(*args)
        outs = pl.pallas_call(
            hand_over,
            out_shape=[jax.ShapeDtypeStruct((width, tokens), BF)] * 2,
            in_specs=[pl.BlockSpec(memory_space=pl.ANY)] * 2,
            out_specs=[pl.BlockSpec(memory_space=pl.ANY)] * 2,
            scratch_shapes=[vm(width, tokens)] * 2 + [dma((4,))],
            name="hand_over",
        )(*outs)
        return tuple(o.T[None] for o in outs)

    return jax.shard_map(
        shards,
        mesh=mesh,
        in_specs=(P("section", "dev", "node"), P("section", "dev", None), P("section", "dev", None)) * 2
        + (P("section", "dev", "node", None),) * 2
        + (P("section", "dev", None, "node"),)
        + (P("section", "dev", None, None),) * 2,
        out_specs=(P("section", "dev", "node"), P("section", "dev", "node")),
        check_vma=False,
    )
```
